32 devices in a mesh: vocab: 4 (over z), seq: 2 (over x), width: 4 (over y, core).
Axes of the slice: x: 2, y: 2, z: 4, core: 2. Of those that a mesh axis runs over, the one named last changes fastest.
Arguments:
- hidden_states: bfloat16 [1024, 5376], P(('vocab', 'seq'), 'width'), may hold values from -8 to 8
- embedding: bfloat16 [256, 5376], P(('vocab', 'seq'), 'width'), may hold values from -5 to 5
- momentum: float32 [256, 5376], P(('vocab', 'seq'), 'width'), may hold values from -2.5 to 2.5
- input_grad: bfloat16 [1024, 5376], P(('vocab', 'seq'), 'width'), may hold values from -0.01953125 to 0.01953125
- rest_lse: float32 [1024], replicated, may hold values from 9 to 13
- targets: int32 [1024], replicated, may hold values from 0 to 255
- owner_of_token: int32 [1024, 1], replicated, may hold values from 0 to 7; in each aligned block of 128 rows (0 to 127, 128 to 255, ...) at most 32 rows name the same one
- row_in_owner: int32 [1024], replicated, may hold values from 0 to 31
Outputs:
- token_loss: float32 [1024], P(('vocab', 'seq', 'width'))
- new_momentum: float32 [256, 5376], P(('vocab', 'seq'), 'width')
- new_embedding: bfloat16 [256, 5376], P(('vocab', 'seq'), 'width')
The draws below stay inside these ranges and needn't reach their ends.
Inputs may be any that keep to these rules, and one draw needn't show every extreme that they name: `owner_of_token`: in each aligned block of 128 tokens (the tokens of one device) no value is named more than 32 times.
All inputs are finite; a program needn't handle non-finite values.
Results may differ from the reference program's by a relative error of at most 0.00068.
Values may be sent and summed in bfloat16 or wider, within the bound.
A program may use at most 64 MiB of HBM per device.

```python
import math
import jax
import jax.numpy as jnp
import numpy as np
from jax import lax

D = 5376
TOK_DEV = 128
ROWS_DEV = 32
CAP = 32
VOCAB = 256
TOKENS = 1024
N_VOCAB = 4
N_SEQ = 2


def embedding_base(key):
    normal_draw = jax.random.normal(jax.random.fold_in(key, 11), (VOCAB, D), jnp.float32)
    return jnp.clip(normal_draw, -5.0, 5.0)


def draw_embedding(key, part):
    base_rows = embedding_base(key)
    return base_rows.astype(jnp.bfloat16)


def draw_hidden_states(key, part):
    normal_draw = jax.random.normal(jax.random.fold_in(key, 12), (TOKENS, D), jnp.float32)
    spread = 3.0 / math.sqrt(D)
    states = spread * normal_draw
    return jnp.clip(states, -8.0, 8.0).astype(jnp.bfloat16)


def draw_momentum(key, part):
    row_spread = jnp.power(10.0, jax.random.uniform(jax.random.fold_in(key, 22), (VOCAB, 1), jnp.float32))
    position = jnp.arange(D, dtype=jnp.float32)[None, :] / (D - 1)
    rough = jnp.power(10.0, 0.3 * jax.random.uniform(jax.random.fold_in(key, 23), (1, D), jnp.float32))
    values = jnp.clip(jax.random.normal(jax.random.fold_in(key, 21), (VOCAB, D), jnp.float32), -2.5, 2.5)
    col_spread = jnp.power(10.0, position) * rough
    factor = 0.005
    return factor * values * row_spread * col_spread


def plant(entries, stream_key, smallest, largest):
    longest = entries.shape.index(max(entries.shape))
    spots = []
    for shift in (0, 1):
        where = [jax.random.randint(jax.random.fold_in(stream_key, axis), (), 0, length) for axis, length in enumerate(entries.shape)]
        where[longest] = (where[longest] + shift) % entries.shape[longest]
        spots.append(tuple(where))
    return entries.at[spots[0]].set(smallest).at[spots[1]].set(largest)


def level_of(stream_key, extent, shards, least, top_value):
    def one(axis_at, parts):
        draws = jax.random.uniform(jax.random.fold_in(jax.random.fold_in(stream_key, 6), axis_at), (parts,), jnp.float32, least / len(shards), top_value / len(shards))
        return jnp.repeat(jnp.exp(draws), extent[axis_at] // parts).reshape((-1,) + (1,) * (len(extent) - axis_at - 1))

    gain = one(*shards[0])
    for cut in shards[1:]:
        gain = gain * one(*cut)
    return gain


def rank_bounds(number_of, skew):
    portions = [(1 << 20) // math.isqrt(rank ** skew) + 1 for rank in range(1, number_of + 1)]
    width = 1 + sum(portions) // (1 << 30)
    return np.cumsum(np.array([max(1, weight // width) for weight in portions]))


def ranked(stream_key, dims, count, lean):
    listing = rank_bounds(count, lean)
    lot = jax.random.randint(jax.random.fold_in(stream_key, 1), dims, 0, int(listing[count - 1]))
    standing = jnp.searchsorted(jnp.asarray(listing, jnp.int32), lot, side="right")
    return jax.random.permutation(jax.random.fold_in(stream_key, 2), count)[standing].astype(jnp.int32)


def shared_out(key, own, number, rows, number_of, top, limit, lean):
    ranking = jax.random.permutation(key, number_of)
    heavy_load, usual = shares(number_of, rows * top, limit, lean, True), shares(number_of, rows * top, limit, lean, False)
    places = jnp.arange(number_of)

    def named(tallies, rotation):
        used = int((tallies > 0).sum())
        fixed = max(1, used // 4)
        passed = fixed + (places - fixed + rotation * (used - fixed)) % max(1, number_of - fixed)
        return jnp.zeros((number_of,), jnp.int32).at[ranking[jnp.where(places < fixed, places, passed)]].set(jnp.asarray(tallies, jnp.int32))

    tallies = jnp.where(number % 4 == 0, named(heavy_load, number // 4), named(usual, number - number // 4 - 1))
    mixed = jax.random.permutation(jax.random.fold_in(own, 3), number_of)
    donor, taker = mixed[0:number_of // 2 * 2:2], mixed[1:number_of // 2 * 2:2]
    room = jnp.minimum(tallies[donor] - 1, limit - tallies[taker]) // 2
    room = jnp.where((donor == ranking[0]) | (taker == ranking[0]) | (tallies[taker] == 0), 0, jnp.maximum(room, 0))
    passed = jax.random.randint(jax.random.fold_in(own, 4), (number_of // 2,), 0, 1 << 20) % (room + 1)
    tallies = tallies.at[donor].add(-passed).at[taker].add(passed)
    items = jnp.searchsorted(jnp.cumsum(tallies), jnp.arange(rows * top), side="right").astype(jnp.int32)
    listing = items.reshape(top, rows).T
    listing = listing[jax.random.permutation(jax.random.fold_in(own, 1), rows)]
    rotation = jax.random.randint(jax.random.fold_in(own, 2), (rows, 1), 0, top)
    return jnp.take_along_axis(listing, (jnp.arange(top)[None, :] + rotation) % top, axis=1)


def shares(number_of, total, most, skew, full):
    portions = [(1 << 20) // math.isqrt(rank ** skew) + 1 for rank in range(1, number_of + 1)]
    largest = most if full else min(most, max(-(-total // number_of), total * portions[0] // sum(portions)))
    least = 1 if total - largest >= number_of - 1 else 0
    given, spare = [largest] + [least] * (number_of - 1), total - largest - least * (number_of - 1)
    while spare > 0:
        free = [i for i in range(1, number_of) if given[i] < largest] or [i for i in range(1, number_of) if given[i] < most]
        mass, budget = sum([portions[i] for i in free]), spare
        for i in free:
            extra = min(most - given[i], max(1, budget * portions[i] // mass), spare)
            given[i] = given[i] + extra
            spare = spare - extra
    return np.array(given)


def bell_draw(stream_key, extent, scale, limit, shards=(), kind=jnp.bfloat16):
    values = scale * jax.random.normal(stream_key, extent, jnp.float32)
    if shards:
        values = values * level_of(stream_key, extent, shards, -0.22, 0.18)
    return jnp.clip(values, -limit, limit).astype(kind)


def setup_inputs(seed: int = 0) -> dict:
    keys = jax.random.split(jax.random.key(seed), 9)
    hidden_states = draw_hidden_states(jax.random.fold_in(keys[8], 71), 0)
    embedding = draw_embedding(jax.random.fold_in(keys[8], 71), 0)
    momentum = draw_momentum(jax.random.fold_in(keys[8], 71), 0)
    input_grad = bell_draw(keys[3], (TOKENS, D), 0.0014, 0.01953125, ((0, 8), (1, 4)))
    rest_lse = jnp.clip(jax.random.uniform(keys[4], (TOKENS,), jnp.float32, 9.0, 13.0), 9.0, 13.0)
    targets = plant(ranked(keys[5], (TOKENS,), VOCAB, 2), jax.random.fold_in(keys[5], 3), 0, VOCAB - 1).astype(jnp.int32)
    owner_of_token_keys = jax.random.split(jax.random.fold_in(keys[6], 1), TOKENS // TOK_DEV)
    owner_of_token_turns = jax.random.permutation(jax.random.fold_in(keys[6], 3), TOKENS // TOK_DEV)
    owner_of_token = jax.vmap(lambda own, number: shared_out(jax.random.fold_in(keys[6], 2), own, number, TOK_DEV, N_VOCAB * N_SEQ, 1, CAP, 2))(owner_of_token_keys, owner_of_token_turns).reshape((TOKENS, 1))
    row_in_owner = plant(jax.random.randint(keys[7], (TOKENS,), 0, ROWS_DEV), jax.random.fold_in(keys[7], 1), 0, ROWS_DEV - 1).astype(jnp.int32)
    return {"hidden_states": hidden_states, "embedding": embedding, "momentum": momentum, "input_grad": input_grad, "rest_lse": rest_lse, "targets": targets, "owner_of_token": owner_of_token, "row_in_owner": row_in_owner}


momentum_decay = 0.75
step_size = 0.1
epsilon = 1e-06

def reference(hidden_states, embedding, momentum, input_grad, rest_lse, targets, owner_of_token, row_in_owner):
    vocab_rows = embedding.shape[0]
    block_len = min(1024, TOKENS)
    blocks = TOKENS // block_len
    columns = jnp.arange(vocab_rows, dtype=jnp.int32)
    table_rows = embedding.T

    def one_block(grad_total, inputs):
        states, rest_vals, target_ids = inputs
        logits = jnp.dot(states, table_rows, preferred_element_type=jnp.float32)
        row_top = jnp.maximum(rest_vals, lax.optimization_barrier(jnp.max(logits, axis=1)))
        row_sum = jnp.exp(rest_vals - row_top) + lax.optimization_barrier(jnp.sum(jnp.exp(logits - row_top[:, None]), axis=1))
        log_total = row_top + jnp.log(row_sum)
        matches = columns[None, :] == target_ids[:, None]
        picked = lax.optimization_barrier(jnp.sum(jnp.where(matches, logits, jnp.zeros_like(logits)), axis=1))
        probs_grad = (jnp.exp(logits - log_total[:, None]) - matches.astype(jnp.float32)).astype(jnp.bfloat16)
        grad_total = grad_total + jnp.dot(probs_grad.T, states, preferred_element_type=jnp.float32)
        return (grad_total, log_total - picked)
    inputs = (hidden_states.reshape(blocks, block_len, D), rest_lse.reshape(blocks, block_len), targets.reshape(blocks, block_len))
    grad_logit, losses = lax.scan(one_block, jnp.zeros((vocab_rows, D), jnp.float32), inputs)
    token_loss = losses.reshape(TOKENS)
    token_ids = (owner_of_token[:, 0] * ROWS_DEV + row_in_owner).astype(jnp.int32)
    incidence = jax.ops.segment_sum(input_grad.astype(jnp.float32), token_ids, num_segments=vocab_rows)
    grad = grad_logit + math.sqrt(D) * incidence
    new_momentum = momentum_decay * momentum + (1.0 - momentum_decay) * grad
    row_scale = jnp.sqrt(lax.optimization_barrier(jnp.mean(new_momentum * new_momentum, axis=1, keepdims=True)) + epsilon)
    new_embedding = (embedding.astype(jnp.float32) - step_size * new_momentum / row_scale).astype(jnp.bfloat16)
    return (token_loss, new_momentum, new_embedding)
```

```python
import functools
import math

import jax
import jax.numpy as jnp
from jax import lax
from jax.experimental import pallas as pl
from jax.experimental.pallas import tpu as pltpu
from jax.sharding import PartitionSpec as P

momentum_decay = 0.75
step_size = 0.1
epsilon = 1e-06
MESH = pl.DeviceIdType.MESH
F32 = jnp.float32


def column_of(row):
    n = row.shape[1]
    return jnp.transpose(jnp.broadcast_to(row, (n, n)))


def cuts_of(wide):
    first = wide // 256 * 128
    return ((0, first), (first, wide - first))


def room_for(n):
    return n // 128 * 128 + 128


TOP = 32704.0
STEPS = 64.0


def scale_of(code):
    return jnp.exp2(code * (1.0 / STEPS))


def encode(x, out):
    n = x.shape[1]
    largest = jnp.max(jnp.abs(x), axis=1, keepdims=True)
    code = jnp.ceil(jnp.log2(jnp.maximum(largest, 1e-30)) * STEPS) + 1.0
    out[:, :n] = jnp.round(x * (TOP / scale_of(code))).astype(jnp.int32).astype(jnp.int16)
    wide = jnp.broadcast_to(code, (x.shape[0], out.shape[1] - n))
    out[:, n:] = wide.astype(jnp.int32).astype(jnp.int16)


def decode(x, n):
    code = x[:, n : n + 1].astype(jnp.int32).astype(F32)
    return x[:, :n].astype(jnp.int32).astype(F32) * (scale_of(code) * (1.0 / TOP))


def kernel(
    sizes, hid, emb, mom, ig, rest_h, tgt_h, own_h, row_h, loss_o, grad_o, scale_o,
    rest, tgt, own, row, H, G, E, M, L, Lr, Ps, Pr, part_a, part_b, enc_a, enc_b, recv_a, recv_b, sq, sqr, tcol, rcol,
    h_s, h_r, g_s, g_r, e_s, e_r, l_s, l_r, p_s, p_r, r_s, r_r, q_s, q_r, in_s,
):
    n_v, n_s, n_w = sizes
    v, s, w = lax.axis_index("vocab"), lax.axis_index("seq"), lax.axis_index("width")
    wide, tok = hid.shape
    R = emb.shape[0]
    C = n_v * R
    q = tok // n_w
    cuts = cuts_of(wide)
    part, enc, recv = (part_a, part_b), (enc_a, enc_b), (recv_a, recv_b)
    plane = [(d, e) for d in range(n_s) for e in range(n_w) if (d, e) != (0, 0)]

    def vp(d):
        return lax.rem(v + d + n_v, n_v)

    def sp(d):
        return lax.rem(s + d + n_s, n_s)

    def wp(e):
        return lax.rem(w + e + n_w, n_w)

    barrier = pltpu.get_barrier_semaphore()
    for d, e in plane:
        pl.semaphore_signal(barrier, inc=1, device_id=(v, sp(d), wp(e)), device_id_type=MESH)
    for d in range(1, n_v):
        pl.semaphore_signal(barrier, inc=1, device_id=(vp(d), s, w), device_id_type=MESH)
    local = [
        pltpu.make_async_copy(src, dst, in_s.at[i])
        for i, (src, dst) in enumerate(
            (
                (tgt_h, tgt), (rest_h, rest), (own_h, own), (row_h, row),
                (emb, E.at[v]), (hid, H.at[0]), (ig, G.at[0]), (mom, M),
            )
        )
    ]
    for c in local:
        c.start()
    mine = v * n_s + s
    for c in local[:2]:
        c.wait()
    tcol[...] = column_of(tgt[pl.ds(mine, 1), :])
    rcol[...] = column_of(rest[pl.ds(mine, 1), :])
    pl.semaphore_wait(barrier, len(plane) + n_v - 1)

    def send(src, dst, ss, rs, dev):
        c = pltpu.make_async_remote_copy(
            src_ref=src, dst_ref=dst, send_sem=ss, recv_sem=rs, device_id=dev, device_id_type=MESH
        )
        c.start()
        return c

    ch = {d: send(hid, H.at[d], h_s.at[d], h_r.at[d], (v, sp(d), w)) for d in range(1, n_s)}
    ce = {d: send(emb, E.at[v], e_s.at[d], e_r.at[d], (vp(d), s, w)) for d in range(1, n_v)}

    def one_hot(d):
        block = v * n_s + sp(-d)
        ids = own[pl.ds(block, 1), :] * R + row[pl.ds(block, 1), :]
        r_ids = lax.broadcasted_iota(jnp.int32, (R, tok), 0)
        return jnp.concatenate(
            [(r_ids + (k * n_s + s) * R == ids).astype(F32) for k in range(n_v)], axis=0
        ).astype(jnp.bfloat16)

    cg = {}

    def send_inputs(i):
        at, n = cuts[i]
        for f in range(1, n_s):
            cg[f, i] = send(
                ig.at[pl.ds(at, n)], G.at[f, pl.ds(at, n)],
                g_s.at[f * 2 + i], g_r.at[f * 2 + i], (v, sp(f), w),
            )

    scale = math.sqrt(wide * n_w)

    def input_term(d, i):
        at, n = cuts[i]
        term = scale * lax.dot_general(
            one_hot(d), G[d, at : at + n, :], (((1,), (1,)), ((), ())), preferred_element_type=F32
        )
        part[i][...] = term if d == 0 else part[i][...] + term

    for c in local[2:]:
        c.wait()
    for i in range(len(cuts)):
        input_term(0, i)
    for d in range(1, n_v):
        ce[d].wait_recv()
    table = E[...].reshape(C, wide)
    cl = {}
    for d in range(n_s):
        if d:
            ch[d].wait_recv()
        L[d] = jnp.transpose(jnp.dot(table, H[d], preferred_element_type=F32))
        for e in range(n_w):
            if (d, e) != (0, 0):
                cl[d, e] = send(
                    L.at[d, pl.ds(wp(e) * q, q)], Lr.at[d, e],
                    l_s.at[d * n_w + e], l_r.at[d * n_w + e], (v, sp(-d), wp(e)),
                )

    send_inputs(0)
    logits = []
    for d in range(n_s):
        total = None
        for e in range(n_w):
            if (d, e) == (0, 0):
                x = L[0, pl.ds(w * q, q), :]
            else:
                cl[d, e].wait_recv()
                x = Lr[d, e]
            total = x if total is None else total + x
        logits.append(total)
    t_col = tcol[pl.ds(w * q, q), 0:1]
    rest_col = rcol[pl.ds(w * q, q), 0:1]
    top = rest_col
    for x in logits:
        top = jnp.maximum(top, jnp.max(x, axis=1, keepdims=True))
    row_sum = jnp.exp(rest_col - top)
    picked = jnp.zeros_like(top)
    lane = lax.broadcasted_iota(jnp.int32, (q, C), 1)
    hits = []
    for d, x in enumerate(logits):
        first = jnp.zeros_like(lane)
        for k in range(n_v):
            first = jnp.where(lane >= k * R, (k * n_s + sp(d)) * R - k * R, first)
        hit = lane + first == t_col
        hits.append(hit)
        row_sum = row_sum + jnp.sum(jnp.exp(x - top), axis=1, keepdims=True)
        picked = picked + jnp.sum(jnp.where(hit, x, 0.0), axis=1, keepdims=True)
    log_total = top + jnp.log(row_sum)
    cp = {}
    for d, x in reversed(list(enumerate(logits))):
        grad = (jnp.exp(x - log_total) - jnp.where(hits[d], 1.0, 0.0)).astype(jnp.bfloat16)
        if d == 0:
            Pr[0, pl.ds(w * q, q), :] = grad
            src = Pr.at[0, pl.ds(w * q, q)]
        else:
            Ps[d] = grad
            src = Ps.at[d]
        for e in range(n_w):
            if (d, e) != (0, 0):
                cp[d, e] = send(
                    src, Pr.at[d, pl.ds(w * q, q)],
                    p_s.at[d * n_w + e], p_r.at[d * n_w + e], (v, sp(d), wp(e)),
                )
    send_inputs(1)
    loss = jnp.broadcast_to(log_total - picked, (q, 128))
    loss_o[...] = jnp.transpose(loss)[0:1, :]

    for d, e in plane:
        cp[d, e].wait_recv()
    probs = [jnp.transpose(Pr[d].astype(F32)).astype(jnp.bfloat16) for d in range(n_s)]
    cr = {}
    for i, (at, n) in enumerate(cuts):
        for d in range(n_s):
            if d:
                cg[d, i].wait_recv()
                input_term(d, i)
            part[i][...] += lax.dot_general(
                probs[d], H[d, at : at + n, :], (((1,), (1,)), ((), ())),
                preferred_element_type=F32,
            )
        encode(part[i][...], enc[i])
        for k in range(1, n_v):
            cr[i, k] = send(
                enc[i].at[pl.ds(vp(k) * R, R)], recv[i].at[k],
                r_s.at[i * n_v + k], r_r.at[i * n_v + k], (vp(k), s, w),
            )
    square = jnp.zeros((R, 1), F32)
    for i, (at, n) in enumerate(cuts):
        total = part[i][pl.ds(v * R, R), :]
        for k in range(1, n_v):
            cr[i, k].wait_recv()
            total = total + decode(recv[i][k], n)
        new_mom = momentum_decay * M[:, at : at + n] + (1.0 - momentum_decay) * total
        grad_o[:, at : at + n] = total
        square = square + jnp.sum(new_mom * new_mom, axis=1, keepdims=True)
    sq[...] = jnp.broadcast_to(square, (R, 128))
    cq = {e: send(sq, sqr.at[e], q_s.at[e], q_r.at[e], (v, s, wp(e))) for e in range(1, n_w)}
    squares = sq[...]
    for e in range(1, n_w):
        cq[e].wait_recv()
        squares = squares + sqr[e]
    scale_o[...] = jnp.sqrt(squares / (wide * n_w) + epsilon)
    for group in (ce, ch, cg, cl, cp, cr, cq):
        for c in group.values():
            c.wait_send()


def body(hid, emb, mom, ig, rest, tgt, own, row):
    sizes = tuple(lax.axis_size(a) for a in ("vocab", "seq", "width"))
    n_v, n_s, n_w = sizes
    tok, wide = hid.shape
    R = emb.shape[0]
    C, q = n_v * R, tok // n_w
    blocks = n_v * n_s
    vmem = pltpu.VMEM
    dma = pltpu.SemaphoreType.DMA
    counts = (n_s, n_s * 2, n_v, n_s * n_w, n_s * n_w, 2 * n_v, n_w)
    widths = [n for _, n in cuts_of(wide)]
    loss, grad, scale = pl.pallas_call(
        functools.partial(kernel, sizes),
        out_shape=(
            vmem((1, q), F32),
            vmem((R, wide), F32),
            vmem((R, 128), F32),
        ),
        in_specs=[pl.BlockSpec(memory_space=pltpu.HBM)] * 8,
        out_specs=[pl.BlockSpec(memory_space=vmem)] * 3,
        scratch_shapes=[
            vmem((blocks, tok), F32),
            vmem((blocks, tok), jnp.int32),
            vmem((blocks, tok), jnp.int32),
            vmem((blocks, tok), jnp.int32),
            vmem((n_s, wide, tok), jnp.bfloat16),
            vmem((n_s, wide, tok), jnp.bfloat16),
            vmem((n_v, R, wide), jnp.bfloat16),
            vmem((R, wide), F32),
            vmem((n_s, tok, C), F32),
            vmem((n_s, n_w, q, C), F32),
            vmem((n_s, q, C), jnp.bfloat16),
            vmem((n_s, tok, C), jnp.bfloat16),
            vmem((C, widths[0]), F32),
            vmem((C, widths[1]), F32),
            vmem((C, room_for(widths[0])), jnp.int16),
            vmem((C, room_for(widths[1])), jnp.int16),
            vmem((n_v, R, room_for(widths[0])), jnp.int16),
            vmem((n_v, R, room_for(widths[1])), jnp.int16),
            vmem((R, 128), F32),
            vmem((n_w, R, 128), F32),
            vmem((tok, tok), jnp.int32),
            vmem((tok, tok), F32),
        ] + [dma((n,)) for n in counts for _ in range(2)] + [dma((8,))],
        compiler_params=pltpu.CompilerParams(
            collective_id=0, has_side_effects=True, vmem_limit_bytes=60 * 2**20
        ),
    )(
        hid.T, emb, mom, ig.T,
        rest.reshape(blocks, tok), tgt.reshape(blocks, tok),
        own.reshape(blocks, tok), row.reshape(blocks, tok),
    )
    new_mom = momentum_decay * mom + (1.0 - momentum_decay) * grad
    step = step_size * new_mom / scale[:, 0:1]
    new_emb = (emb.astype(F32) - step).astype(jnp.bfloat16)
    return loss.reshape(q), new_mom, new_emb


def solution(mesh):
    placed = P(("vocab", "seq"), "width")
    return jax.shard_map(
        body,
        mesh=mesh,
        in_specs=(placed, placed, placed, placed, P(), P(), P(), P()),
        out_specs=(P(("vocab", "seq", "width")), placed, placed),
        check_vma=False,
    )
```

```python
import functools
import math

import jax
import jax.numpy as jnp
from jax import lax
from jax.experimental import pallas as pl
from jax.experimental.pallas import tpu as pltpu
from jax.sharding import PartitionSpec as P

momentum_decay = 0.75
step_size = 0.1
epsilon = 1e-06
MESH = pl.DeviceIdType.MESH
F32 = jnp.float32
BF16 = jnp.bfloat16
I16 = jnp.int16
TOP = 32704.0
STEPS = 64.0


def column_of(row):
    n = row.shape[1]
    return jnp.transpose(jnp.broadcast_to(row, (n, n)))


def room_for(n):
    return n // 128 * 128 + 128


def scale_of(code):
    return jnp.exp2(code * (1.0 / STEPS))


def encode(x):
    rows, n = x.shape
    largest = jnp.max(jnp.abs(x), axis=1, keepdims=True)
    code = jnp.ceil(jnp.log2(jnp.maximum(largest, 1e-30)) * STEPS) + 1.0
    values = jnp.round(x * (TOP / scale_of(code)))
    return values.astype(jnp.int32).astype(I16), jnp.broadcast_to(
        code, (rows, room_for(n) - n)
    ).astype(jnp.int32).astype(I16)


def decode(x, n):
    code = x[:, n : n + 1].astype(jnp.int32).astype(F32)
    return x[:, :n].astype(jnp.int32).astype(F32) * (scale_of(code) * (1.0 / TOP))


def kernel(
    sizes, hid, emb, mom, ig, rest_h, tgt_h, own_h, row_h, loss_o, grad_o, scale_o,
    rest, tgt, own, row, H, G, E, M, L, Lr, Ps, Pr, part, enc, recv, Te, Tr, Ue, Ur,
    sq, sqr, tcol, rcol,
    h_s, h_r, e_s, e_r, l_s, l_r, p_s, p_r, r_s, r_r, t_s, t_r, u_s, u_r, q_s, q_r, in_s,
):
    n_v, n_s, n_w = sizes
    v, s, w = lax.axis_index("vocab"), lax.axis_index("seq"), lax.axis_index("width")
    wide, tok = hid.shape
    R = emb.shape[0]
    C = n_v * R
    q = tok // n_w
    plane = [(d, e) for d in range(n_s) for e in range(n_w) if (d, e) != (0, 0)]

    def vp(d):
        return lax.rem(v + d + n_v, n_v)

    def sp(d):
        return lax.rem(s + d + n_s, n_s)

    def wp(e):
        return lax.rem(w + e + n_w, n_w)

    barrier = pltpu.get_barrier_semaphore()

    def greet(sem, *device):
        pl.semaphore_signal(sem, inc=1, device_id=device, device_id_type=MESH)

    for d in range(1, n_v):
        greet(barrier, vp(d), s, w)
    for d, e in plane:
        greet(barrier, v, sp(d), wp(e))
    local = [
        pltpu.make_async_copy(src, dst, in_s.at[i])
        for i, (src, dst) in enumerate(
            (
                (own_h, own), (row_h, row), (ig, G), (tgt_h, tgt), (rest_h, rest),
                (emb, E.at[v]), (hid, H.at[0]), (mom, M),
            )
        )
    ]
    for c in local:
        c.start()

    def copy(src, dst, ss, rs, dev):
        return pltpu.make_async_remote_copy(
            src_ref=src, dst_ref=dst, send_sem=ss, recv_sem=rs, device_id=dev, device_id_type=MESH
        )

    def send(*args):
        c = copy(*args)
        c.start()
        return c

    ch = {d: copy(hid, H.at[d], h_s.at[d], h_r.at[d], (v, sp(d), w)) for d in range(1, n_s)}
    ce = {d: copy(emb, E.at[v], e_s.at[d], e_r.at[d], (vp(d), s, w)) for d in range(1, n_v)}

    pl.semaphore_wait(barrier, len(plane) + n_v - 1)
    for c in [*ce.values(), *ch.values()]:
        c.start()

    mine = v * n_s + s
    r_ids = lax.broadcasted_iota(jnp.int32, (R, tok), 0)
    for c in local[:3]:
        c.wait()
    ids = own[pl.ds(mine, 1), :] * R + row[pl.ds(mine, 1), :]
    scale = math.sqrt(wide * n_w)

    def input_rows(d):
        hot = jnp.concatenate(
            [(r_ids + (k * n_s + sp(d)) * R == ids).astype(F32) for k in range(n_v)], axis=0
        ).astype(BF16)
        return scale * lax.dot_general(
            hot, G[...], (((1,), (1,)), ((), ())), preferred_element_type=F32
        )

    for d in range(1, n_s):
        Te[d, :, :wide], Te[d, :, wide:] = encode(input_rows(d))
    part[...] = input_rows(0)
    for c in local[3:]:
        c.wait()
    tcol[...] = column_of(tgt[pl.ds(mine, 1), :])
    rcol[...] = column_of(rest[pl.ds(mine, 1), :])

    for d in range(1, n_v):
        ce[d].wait_recv()
    table = E[...].reshape(C, wide)
    cl = {}
    for d in range(n_s):
        if d:
            ch[d].wait_recv()
        L[d] = jnp.transpose(jnp.dot(table, H[d], preferred_element_type=F32))
        for e in range(n_w):
            if (d, e) != (0, 0):
                cl[d, e] = send(
                    L.at[d, pl.ds(wp(e) * q, q)], Lr.at[d, e],
                    l_s.at[d * n_w + e], l_r.at[d * n_w + e], (v, sp(-d), wp(e)),
                )
    ct = {
        (d, k): send(
            Te.at[d, pl.ds(vp(k) * R, R)], Tr.at[d, k],
            t_s.at[d * n_v + k], t_r.at[d * n_v + k], (vp(k), s, w),
        )
        for d in range(1, n_s)
        for k in range(1, n_v)
    }
    logits = []
    for d in range(n_s):
        total = None
        for e in range(n_w):
            if (d, e) == (0, 0):
                x = L[0, pl.ds(w * q, q), :]
            else:
                cl[d, e].wait_recv()
                x = Lr[d, e]
            total = x if total is None else total + x
        logits.append(total)
    t_col = tcol[pl.ds(w * q, q), 0:1]
    rest_col = rcol[pl.ds(w * q, q), 0:1]
    top = rest_col
    for x in logits:
        top = jnp.maximum(top, jnp.max(x, axis=1, keepdims=True))
    row_sum = jnp.exp(rest_col - top)
    picked = jnp.zeros_like(top)
    lane = lax.broadcasted_iota(jnp.int32, (q, C), 1)
    hits = []
    for d, x in enumerate(logits):
        base = jnp.zeros_like(lane)
        for k in range(n_v):
            base = jnp.where(lane >= k * R, (k * n_s + sp(d)) * R - k * R, base)
        hit = lane + base == t_col
        hits.append(hit)
        row_sum = row_sum + jnp.sum(jnp.exp(x - top), axis=1, keepdims=True)
        picked = picked + jnp.sum(jnp.where(hit, x, 0.0), axis=1, keepdims=True)
    log_total = top + jnp.log(row_sum)
    cp = {}
    for d, x in reversed(list(enumerate(logits))):
        grad = (jnp.exp(x - log_total) - jnp.where(hits[d], 1.0, 0.0)).astype(BF16)
        if d == 0:
            Pr[0, pl.ds(w * q, q), :] = grad
            src = Pr.at[0, pl.ds(w * q, q)]
        else:
            Ps[d] = grad
            src = Ps.at[d]
        for e in range(n_w):
            if (d, e) != (0, 0):
                cp[d, e] = send(
                    src, Pr.at[d, pl.ds(w * q, q)],
                    p_s.at[d * n_w + e], p_r.at[d * n_w + e], (v, sp(d), wp(e)),
                )
    loss = jnp.broadcast_to(log_total - picked, (q, 128))
    loss_o[...] = jnp.transpose(loss)[0:1, :]

    for d, e in plane:
        cp[d, e].wait_recv()
    probs = [jnp.transpose(Pr[d].astype(F32)).astype(BF16) for d in range(n_s)]
    for d in range(n_s):
        part[...] += lax.dot_general(
            probs[d], H[d], (((1,), (1,)), ((), ())), preferred_element_type=F32
        )
    enc[:, :wide], enc[:, wide:] = encode(part[...])
    cr = {}
    for k in range(1, n_v):
        cr[k] = send(
            enc.at[pl.ds(vp(k) * R, R)], recv.at[k], r_s.at[k], r_r.at[k], (vp(k), s, w)
        )

    cu = {}
    for d in range(1, n_s):
        total = decode(Te[d, pl.ds(v * R, R), :], wide)
        for k in range(1, n_v):
            ct[d, k].wait_recv()
            total = total + decode(Tr[d, k], wide)
        Ue[d, :, :wide], Ue[d, :, wide:] = encode(total)
        cu[d] = send(Ue.at[d], Ur.at[d], u_s.at[d], u_r.at[d], (v, sp(d), w))
    total = part[pl.ds(v * R, R), :]
    for d in range(1, n_s):
        cu[d].wait_recv()
        total = total + decode(Ur[d], wide)
    for k in range(1, n_v):
        cr[k].wait_recv()
        total = total + decode(recv[k], wide)
    grad_o[...] = total
    new_mom = momentum_decay * M[...] + (1.0 - momentum_decay) * total
    square = jnp.sum(new_mom * new_mom, axis=1, keepdims=True)
    sq[...] = jnp.broadcast_to(square, (R, 128))
    cq = {e: send(sq, sqr.at[e], q_s.at[e], q_r.at[e], (v, s, wp(e))) for e in range(1, n_w)}
    squares = sq[...]
    for e in range(1, n_w):
        cq[e].wait_recv()
        squares = squares + sqr[e]
    scale_o[...] = jnp.sqrt(squares / (wide * n_w) + epsilon)
    for group in (ce, ch, ct, cl, cp, cr, cu, cq):
        for c in group.values():
            c.wait_send()


def body(hid, emb, mom, ig, rest, tgt, own, row):
    sizes = tuple(lax.axis_size(a) for a in ("vocab", "seq", "width"))
    n_v, n_s, n_w = sizes
    tok, wide = hid.shape
    R = emb.shape[0]
    C, q = n_v * R, tok // n_w
    blocks = n_v * n_s
    room = room_for(wide)
    vmem = pltpu.VMEM
    dma = pltpu.SemaphoreType.DMA
    counts = (n_s, n_v, n_s * n_w, n_s * n_w, n_v, n_s * n_v, n_s, n_w)
    loss, grad, scale = pl.pallas_call(
        functools.partial(kernel, sizes),
        out_shape=(vmem((1, q), F32), vmem((R, wide), F32), vmem((R, 128), F32)),
        in_specs=[pl.BlockSpec(memory_space=pltpu.HBM)] * 8,
        out_specs=[pl.BlockSpec(memory_space=vmem)] * 3,
        scratch_shapes=[
            vmem((blocks, tok), F32),
            vmem((blocks, tok), jnp.int32),
            vmem((blocks, tok), jnp.int32),
            vmem((blocks, tok), jnp.int32),
            vmem((n_s, wide, tok), BF16),
            vmem((wide, tok), BF16),
            vmem((n_v, R, wide), BF16),
            vmem((R, wide), F32),
            vmem((n_s, tok, C), F32),
            vmem((n_s, n_w, q, C), F32),
            vmem((n_s, q, C), BF16),
            vmem((n_s, tok, C), BF16),
            vmem((C, wide), F32),
            vmem((C, room), I16),
            vmem((n_v, R, room), I16),
            vmem((n_s, C, room), I16),
            vmem((n_s, n_v, R, room), I16),
            vmem((n_s, R, room), I16),
            vmem((n_s, R, room), I16),
            vmem((R, 128), F32),
            vmem((n_w, R, 128), F32),
            vmem((tok, tok), jnp.int32),
            vmem((tok, tok), F32),
        ]
        + [dma((n,)) for n in counts for _ in range(2)]
        + [dma((8,))],
        compiler_params=pltpu.CompilerParams(
            collective_id=0, has_side_effects=True, vmem_limit_bytes=60 * 2**20
        ),
    )(
        hid.T, emb, mom, ig.T,
        rest.reshape(blocks, tok), tgt.reshape(blocks, tok),
        own.reshape(blocks, tok), row.reshape(blocks, tok),
    )
    new_mom = momentum_decay * mom + (1.0 - momentum_decay) * grad
    step = step_size * new_mom / scale[:, 0:1]
    new_emb = (emb.astype(F32) - step).astype(BF16)
    return loss.reshape(q), new_mom, new_emb


def solution(mesh):
    placed = P(("vocab", "seq"), "width")
    return jax.shard_map(
        body,
        mesh=mesh,
        in_specs=(placed, placed, placed, placed, P(), P(), P(), P()),
        out_specs=(P(("vocab", "seq", "width")), placed, placed),
        check_vma=False,
    )
```

```python
import functools
import math

import jax
import jax.numpy as jnp
from jax import lax
from jax.experimental import pallas as pl
from jax.experimental.pallas import tpu as pltpu
from jax.sharding import PartitionSpec as P

momentum_decay = 0.75
step_size = 0.1
epsilon = 1e-06
MESH = pl.DeviceIdType.MESH
F32 = jnp.float32
BF16 = jnp.bfloat16
I16 = jnp.int16
TOP = 32704.0
STEPS = 64.0


def column_of(row):
    n = row.shape[1]
    return jnp.transpose(jnp.broadcast_to(row, (n, n)))


def room_for(n):
    return n // 128 * 128 + 128


def scale_of(code):
    return jnp.exp2(code * (1.0 / STEPS))


def encode(x):
    rows, n = x.shape
    largest = jnp.max(jnp.abs(x), axis=1, keepdims=True)
    code = jnp.ceil(jnp.log2(jnp.maximum(largest, 1e-30)) * STEPS) + 1.0
    values = jnp.round(x * (TOP / scale_of(code)))
    return values.astype(jnp.int32).astype(I16), jnp.broadcast_to(
        code, (rows, room_for(n) - n)
    ).astype(jnp.int32).astype(I16)


def decode(x, n):
    code = x[:, n : n + 1].astype(jnp.int32).astype(F32)
    return x[:, :n].astype(jnp.int32).astype(F32) * (scale_of(code) * (1.0 / TOP))


def kernel(
    sizes, hid, emb, mom, ig, rest_h, tgt_h, own_h, row_h, loss_o, grad_o, scale_o,
    rest, tgt, own, row, H, G, E, M, L, Lr, Ps, Pr, part, enc, recv, Te, Tr, Ue, Ur,
    sq, sqr, tcol, rcol,
    h_s, h_r, e_s, e_r, l_s, l_r, p_s, p_r, r_s, r_r, t_s, t_r, u_s, u_r, q_s, q_r, in_s,
    near, far,
):
    n_v, n_s, n_w = sizes
    v, s, w = lax.axis_index("vocab"), lax.axis_index("seq"), lax.axis_index("width")
    wide, tok = hid.shape
    R = emb.shape[0]
    C = n_v * R
    q = tok // n_w
    plane = [(d, e) for d in range(n_s) for e in range(n_w) if (d, e) != (0, 0)]

    def vp(d):
        return lax.rem(v + d + n_v, n_v)

    def sp(d):
        return lax.rem(s + d + n_s, n_s)

    def wp(e):
        return lax.rem(w + e + n_w, n_w)

    barrier = pltpu.get_barrier_semaphore()
    even = lax.rem(w, 2) == 0
    first, last = w - lax.rem(w, 2), w - lax.rem(w, 2) + 1

    def greet(sem, *device):
        pl.semaphore_signal(sem, inc=1, device_id=device, device_id_type=MESH)

    for d in range(1, n_v):
        greet(barrier, vp(d), s, last)

    @pl.when(even)
    def _():
        greet(barrier, v, s, last)
        for d in range(1, n_s):
            greet(barrier, v, sp(d), first)

    @pl.when(jnp.logical_not(even))
    def _():
        for d in range(n_s):
            greet(barrier, v, sp(d), first)

    for e in range(2, n_w, 2):
        for d in range(n_s):
            greet(barrier, v, sp(d), lax.rem(first + e, n_w))

    local = [
        pltpu.make_async_copy(src, dst, in_s.at[i])
        for i, (src, dst) in enumerate(
            (
                (own_h, own), (row_h, row), (ig, G), (tgt_h, tgt), (rest_h, rest),
                (emb, E.at[v]), (hid, H.at[0]), (mom, M),
            )
        )
    ]
    for c in local:
        c.start()

    def copy(src, dst, ss, rs, dev):
        return pltpu.make_async_remote_copy(
            src_ref=src, dst_ref=dst, send_sem=ss, recv_sem=rs, device_id=dev, device_id_type=MESH
        )

    def send(*args):
        c = copy(*args)
        c.start()
        return c

    ch = {d: copy(hid, H.at[d], h_s.at[d], h_r.at[d], (v, sp(d), w)) for d in range(1, n_s)}
    ce = {d: copy(emb, E.at[v], e_s.at[d], e_r.at[d], (vp(d), s, w)) for d in range(1, n_v)}

    @pl.when(even)
    def _():
        pl.semaphore_wait(barrier, n_s * n_w - 1)
        greet(near, v, s, last)
        for c in ch.values():
            c.start()
        pl.semaphore_wait(far, 1)
        for c in ce.values():
            c.start()

    @pl.when(jnp.logical_not(even))
    def _():
        pl.semaphore_wait(barrier, 2 * n_v - 1)
        greet(far, v, s, first)
        for c in ce.values():
            c.start()
        pl.semaphore_wait(near, 1)
        for c in ch.values():
            c.start()

    mine = v * n_s + s
    r_ids = lax.broadcasted_iota(jnp.int32, (R, tok), 0)
    for c in local[:3]:
        c.wait()
    ids = own[pl.ds(mine, 1), :] * R + row[pl.ds(mine, 1), :]
    scale = math.sqrt(wide * n_w)

    def input_rows(d):
        hot = jnp.concatenate(
            [(r_ids + (k * n_s + sp(d)) * R == ids).astype(F32) for k in range(n_v)], axis=0
        ).astype(BF16)
        return scale * lax.dot_general(
            hot, G[...], (((1,), (1,)), ((), ())), preferred_element_type=F32
        )

    for d in range(1, n_s):
        Te[d, :, :wide], Te[d, :, wide:] = encode(input_rows(d))
    part[...] = input_rows(0)
    for c in local[3:]:
        c.wait()
    tcol[...] = column_of(tgt[pl.ds(mine, 1), :])
    rcol[...] = column_of(rest[pl.ds(mine, 1), :])

    for d in range(1, n_v):
        ce[d].wait_recv()
    table = E[...].reshape(C, wide)
    cl = {}
    for d in range(n_s):
        if d:
            ch[d].wait_recv()
        L[d] = jnp.transpose(jnp.dot(table, H[d], preferred_element_type=F32))
        for e in range(n_w):
            if (d, e) != (0, 0):
                cl[d, e] = send(
                    L.at[d, pl.ds(wp(e) * q, q)], Lr.at[d, e],
                    l_s.at[d * n_w + e], l_r.at[d * n_w + e], (v, sp(-d), wp(e)),
                )
    ct = {
        (d, k): send(
            Te.at[d, pl.ds(vp(k) * R, R)], Tr.at[d, k],
            t_s.at[d * n_v + k], t_r.at[d * n_v + k], (vp(k), s, w),
        )
        for d in range(1, n_s)
        for k in range(1, n_v)
    }
    logits = []
    for d in range(n_s):
        total = None
        for e in range(n_w):
            if (d, e) == (0, 0):
                x = L[0, pl.ds(w * q, q), :]
            else:
                cl[d, e].wait_recv()
                x = Lr[d, e]
            total = x if total is None else total + x
        logits.append(total)
    t_col = tcol[pl.ds(w * q, q), 0:1]
    rest_col = rcol[pl.ds(w * q, q), 0:1]
    top = rest_col
    for x in logits:
        top = jnp.maximum(top, jnp.max(x, axis=1, keepdims=True))
    row_sum = jnp.exp(rest_col - top)
    picked = jnp.zeros_like(top)
    lane = lax.broadcasted_iota(jnp.int32, (q, C), 1)
    hits = []
    for d, x in enumerate(logits):
        base = jnp.zeros_like(lane)
        for k in range(n_v):
            base = jnp.where(lane >= k * R, (k * n_s + sp(d)) * R - k * R, base)
        hit = lane + base == t_col
        hits.append(hit)
        row_sum = row_sum + jnp.sum(jnp.exp(x - top), axis=1, keepdims=True)
        picked = picked + jnp.sum(jnp.where(hit, x, 0.0), axis=1, keepdims=True)
    log_total = top + jnp.log(row_sum)
    cp = {}
    for d, x in reversed(list(enumerate(logits))):
        grad = (jnp.exp(x - log_total) - jnp.where(hits[d], 1.0, 0.0)).astype(BF16)
        if d == 0:
            Pr[0, pl.ds(w * q, q), :] = grad
            src = Pr.at[0, pl.ds(w * q, q)]
        else:
            Ps[d] = grad
            src = Ps.at[d]
        for e in range(n_w):
            if (d, e) != (0, 0):
                cp[d, e] = send(
                    src, Pr.at[d, pl.ds(w * q, q)],
                    p_s.at[d * n_w + e], p_r.at[d * n_w + e], (v, sp(d), wp(e)),
                )
    loss = jnp.broadcast_to(log_total - picked, (q, 128))
    loss_o[...] = jnp.transpose(loss)[0:1, :]

    for d, e in plane:
        cp[d, e].wait_recv()
    probs = [jnp.transpose(Pr[d].astype(F32)).astype(BF16) for d in range(n_s)]
    for d in range(n_s):
        part[...] += lax.dot_general(
            probs[d], H[d], (((1,), (1,)), ((), ())), preferred_element_type=F32
        )
    enc[:, :wide], enc[:, wide:] = encode(part[...])
    cr = {}
    for k in range(1, n_v):
        cr[k] = send(
            enc.at[pl.ds(vp(k) * R, R)], recv.at[k], r_s.at[k], r_r.at[k], (vp(k), s, w)
        )

    cu = {}
    for d in range(1, n_s):
        total = decode(Te[d, pl.ds(v * R, R), :], wide)
        for k in range(1, n_v):
            ct[d, k].wait_recv()
            total = total + decode(Tr[d, k], wide)
        Ue[d, :, :wide], Ue[d, :, wide:] = encode(total)
        cu[d] = send(Ue.at[d], Ur.at[d], u_s.at[d], u_r.at[d], (v, sp(d), w))
    total = part[pl.ds(v * R, R), :]
    for d in range(1, n_s):
        cu[d].wait_recv()
        total = total + decode(Ur[d], wide)
    for k in range(1, n_v):
        cr[k].wait_recv()
        total = total + decode(recv[k], wide)
    grad_o[...] = total
    new_mom = momentum_decay * M[...] + (1.0 - momentum_decay) * total
    square = jnp.sum(new_mom * new_mom, axis=1, keepdims=True)
    sq[...] = jnp.broadcast_to(square, (R, 128))
    cq = {e: send(sq, sqr.at[e], q_s.at[e], q_r.at[e], (v, s, wp(e))) for e in range(1, n_w)}
    squares = sq[...]
    for e in range(1, n_w):
        cq[e].wait_recv()
        squares = squares + sqr[e]
    factor = step_size / jnp.sqrt(squares[:, 0:1] / (wide * n_w) + epsilon)
    scale_o[...] = jnp.broadcast_to(factor, (R, wide))
    for group in (ce, ch, ct, cl, cp, cr, cu, cq):
        for c in group.values():
            c.wait_send()


def body(hid, emb, mom, ig, rest, tgt, own, row):
    sizes = tuple(lax.axis_size(a) for a in ("vocab", "seq", "width"))
    n_v, n_s, n_w = sizes
    tok, wide = hid.shape
    R = emb.shape[0]
    C, q = n_v * R, tok // n_w
    blocks = n_v * n_s
    room = room_for(wide)
    vmem = pltpu.VMEM
    dma = pltpu.SemaphoreType.DMA
    counts = (n_s, n_v, n_s * n_w, n_s * n_w, n_v, n_s * n_v, n_s, n_w)
    loss, grad, scale = pl.pallas_call(
        functools.partial(kernel, sizes),
        out_shape=(vmem((1, q), F32), vmem((R, wide), F32), vmem((R, wide), F32)),
        in_specs=[pl.BlockSpec(memory_space=pltpu.HBM)] * 8,
        out_specs=[pl.BlockSpec(memory_space=vmem)] * 3,
        scratch_shapes=[
            vmem((blocks, tok), F32),
            vmem((blocks, tok), jnp.int32),
            vmem((blocks, tok), jnp.int32),
            vmem((blocks, tok), jnp.int32),
            vmem((n_s, wide, tok), BF16),
            vmem((wide, tok), BF16),
            vmem((n_v, R, wide), BF16),
            vmem((R, wide), F32),
            vmem((n_s, tok, C), F32),
            vmem((n_s, n_w, q, C), F32),
            vmem((n_s, q, C), BF16),
            vmem((n_s, tok, C), BF16),
            vmem((C, wide), F32),
            vmem((C, room), I16),
            vmem((n_v, R, room), I16),
            vmem((n_s, C, room), I16),
            vmem((n_s, n_v, R, room), I16),
            vmem((n_s, R, room), I16),
            vmem((n_s, R, room), I16),
            vmem((R, 128), F32),
            vmem((n_w, R, 128), F32),
            vmem((tok, tok), jnp.int32),
            vmem((tok, tok), F32),
        ]
        + [dma((n,)) for n in counts for _ in range(2)]
        + [dma((8,)), pltpu.SemaphoreType.REGULAR, pltpu.SemaphoreType.REGULAR],
        compiler_params=pltpu.CompilerParams(
            collective_id=0, has_side_effects=True, vmem_limit_bytes=60 * 2**20
        ),
    )(
        hid.T, emb, mom, ig.T,
        rest.reshape(blocks, tok), tgt.reshape(blocks, tok),
        own.reshape(blocks, tok), row.reshape(blocks, tok),
    )
    new_mom = momentum_decay * mom + (1.0 - momentum_decay) * grad
    new_emb = (emb.astype(F32) - scale * new_mom).astype(BF16)
    return loss.reshape(q), new_mom, new_emb


def solution(mesh):
    placed = P(("vocab", "seq"), "width")
    return jax.shard_map(
        body,
        mesh=mesh,
        in_specs=(placed, placed, placed, placed, P(), P(), P(), P()),
        out_specs=(P(("vocab", "seq", "width")), placed, placed),
        check_vma=False,
    )
```

```python
import functools
import math

import jax
import jax.numpy as jnp
from jax import lax
from jax.experimental import pallas as pl
from jax.experimental.pallas import tpu as pltpu
from jax.sharding import PartitionSpec as P

momentum_decay = 0.75
step_size = 0.1
epsilon = 1e-06
MESH = pl.DeviceIdType.MESH
F32 = jnp.float32
BF16 = jnp.bfloat16
I16 = jnp.int16
TOP = 32704.0
STEPS = 64.0


def column_of(row):
    n = row.shape[1]
    return jnp.transpose(jnp.broadcast_to(row, (n, n)))


def room_for(n):
    return n // 128 * 128 + 128


def scale_of(code):
    return jnp.exp2(code * (1.0 / STEPS))


def encode(x):
    rows, n = x.shape
    largest = jnp.max(jnp.abs(x), axis=1, keepdims=True)
    code = jnp.ceil(jnp.log2(jnp.maximum(largest, 1e-30)) * STEPS) + 1.0
    values = jnp.round(x * (TOP / scale_of(code)))
    return values.astype(jnp.int32).astype(I16), jnp.broadcast_to(
        code, (rows, room_for(n) - n)
    ).astype(jnp.int32).astype(I16)


def decode(x, n):
    code = x[:, n : n + 1].astype(jnp.int32).astype(F32)
    return x[:, :n].astype(jnp.int32).astype(F32) * (scale_of(code) * (1.0 / TOP))


def kernel(
    sizes, hid, emb, mom, ig, rest_h, tgt_h, own_h, row_h, loss_o, grad_o, scale_o,
    rest, tgt, own, row, H, G, E, M, L, Lr, Ps, Pr, part, enc, recv, Te, Tr, Ue, Ur,
    sq, sqr, tcol, rcol,
    h_s, h_r, e_s, e_r, l_s, l_r, p_s, p_r, r_s, r_r, t_s, t_r, u_s, u_r, q_s, q_r, in_s,
    near, far,
):
    n_v, n_s, n_w = sizes
    v, s, w = lax.axis_index("vocab"), lax.axis_index("seq"), lax.axis_index("width")
    wide, tok = hid.shape
    R = emb.shape[0]
    C = n_v * R
    q = tok // n_w
    plane = [(d, e) for d in range(n_s) for e in range(n_w) if (d, e) != (0, 0)]

    by_reach = sorted(range(n_w), key=lambda e: -(e // 2))

    def vp(d):
        return lax.rem(v + d + n_v, n_v)

    def sp(d):
        return lax.rem(s + d + n_s, n_s)

    def wp(e):
        pair = lax.rem(lax.div(w, 2) + e // 2, n_w // 2)
        return pair * 2 + lax.rem(w + e % 2, 2)

    barrier = pltpu.get_barrier_semaphore()
    even = lax.rem(w, 2) == 0
    first, last = w - lax.rem(w, 2), w - lax.rem(w, 2) + 1

    def greet(sem, *device):
        pl.semaphore_signal(sem, inc=1, device_id=device, device_id_type=MESH)

    for d in range(1, n_v):
        greet(barrier, vp(d), s, last)

    @pl.when(even)
    def _():
        greet(barrier, v, s, last)
        for d in range(1, n_s):
            greet(barrier, v, sp(d), first)

    @pl.when(jnp.logical_not(even))
    def _():
        for d in range(n_s):
            greet(barrier, v, sp(d), first)

    for e in range(2, n_w, 2):
        for d in range(n_s):
            greet(barrier, v, sp(d), lax.rem(last + e, n_w))

    local = [
        pltpu.make_async_copy(src, dst, in_s.at[i])
        for i, (src, dst) in enumerate(
            (
                (own_h, own), (row_h, row), (ig, G), (tgt_h, tgt), (rest_h, rest),
                (emb, E.at[v]), (hid, H.at[0]), (mom, M),
            )
        )
    ]
    for c in local:
        c.start()

    def copy(src, dst, ss, rs, dev):
        return pltpu.make_async_remote_copy(
            src_ref=src, dst_ref=dst, send_sem=ss, recv_sem=rs, device_id=dev, device_id_type=MESH
        )

    def send(*args):
        c = copy(*args)
        c.start()
        return c

    ch = {d: copy(hid, H.at[d], h_s.at[d], h_r.at[d], (v, sp(d), w)) for d in range(1, n_s)}
    ce = {d: copy(emb, E.at[v], e_s.at[d], e_r.at[d], (vp(d), s, w)) for d in range(1, n_v)}

    @pl.when(even)
    def _():
        pl.semaphore_wait(barrier, 2 * n_s - 1)
        greet(near, v, s, last)

    @pl.when(jnp.logical_not(even))
    def _():
        pl.semaphore_wait(near, 1)

    for c in ch.values():
        c.start()

    @pl.when(jnp.logical_not(even))
    def _():
        pl.semaphore_wait(barrier, 2 * n_v - 1 + n_s * (n_w - 2))
        greet(far, v, s, first)

    @pl.when(even)
    def _():
        pl.semaphore_wait(far, 1)

    for c in ce.values():
        c.start()

    mine = v * n_s + s
    r_ids = lax.broadcasted_iota(jnp.int32, (R, tok), 0)
    for c in local[:3]:
        c.wait()
    ids = own[pl.ds(mine, 1), :] * R + row[pl.ds(mine, 1), :]
    scale = math.sqrt(wide * n_w)

    def input_rows(d):
        hot = jnp.concatenate(
            [(r_ids + (k * n_s + sp(d)) * R == ids).astype(F32) for k in range(n_v)], axis=0
        ).astype(BF16)
        return scale * lax.dot_general(
            hot, G[...], (((1,), (1,)), ((), ())), preferred_element_type=F32
        )

    for d in range(1, n_s):
        Te[d, :, :wide], Te[d, :, wide:] = encode(input_rows(d))
    part[...] = input_rows(0)
    for c in local[3:]:
        c.wait()
    tcol[...] = column_of(tgt[pl.ds(mine, 1), :])
    rcol[...] = column_of(rest[pl.ds(mine, 1), :])

    for d in range(1, n_v):
        ce[d].wait_recv()
    table = E[...].reshape(C, wide)
    cl = {}
    for d in reversed(range(n_s)):
        if d:
            ch[d].wait_recv()
        L[d] = jnp.transpose(jnp.dot(table, H[d], preferred_element_type=F32))
        for e in by_reach:
            if (d, e) != (0, 0):
                cl[d, e] = send(
                    L.at[d, pl.ds(wp(e) * q, q)], Lr.at[d, e],
                    l_s.at[d * n_w + e], l_r.at[d * n_w + e], (v, sp(-d), wp(e)),
                )
    ct = {
        (d, k): send(
            Te.at[d, pl.ds(vp(k) * R, R)], Tr.at[d, k],
            t_s.at[d * n_v + k], t_r.at[d * n_v + k], (vp(k), s, w),
        )
        for d in range(1, n_s)
        for k in range(1, n_v)
    }
    logits = []
    for d in range(n_s):
        total = None
        for e in range(n_w):
            if (d, e) == (0, 0):
                x = L[0, pl.ds(w * q, q), :]
            else:
                cl[d, e].wait_recv()
                x = Lr[d, e]
            total = x if total is None else total + x
        logits.append(total)
    t_col = tcol[pl.ds(w * q, q), 0:1]
    rest_col = rcol[pl.ds(w * q, q), 0:1]
    top = rest_col
    for x in logits:
        top = jnp.maximum(top, jnp.max(x, axis=1, keepdims=True))
    row_sum = jnp.exp(rest_col - top)
    picked = jnp.zeros_like(top)
    lane = lax.broadcasted_iota(jnp.int32, (q, C), 1)
    hits = []
    for d, x in enumerate(logits):
        base = jnp.zeros_like(lane)
        for k in range(n_v):
            base = jnp.where(lane >= k * R, (k * n_s + sp(d)) * R - k * R, base)
        hit = lane + base == t_col
        hits.append(hit)
        row_sum = row_sum + jnp.sum(jnp.exp(x - top), axis=1, keepdims=True)
        picked = picked + jnp.sum(jnp.where(hit, x, 0.0), axis=1, keepdims=True)
    log_total = top + jnp.log(row_sum)
    cp = {}
    for d, x in reversed(list(enumerate(logits))):
        grad = (jnp.exp(x - log_total) - jnp.where(hits[d], 1.0, 0.0)).astype(BF16)
        if d == 0:
            Pr[0, pl.ds(w * q, q), :] = grad
            src = Pr.at[0, pl.ds(w * q, q)]
        else:
            Ps[d] = grad
            src = Ps.at[d]
        for e in by_reach:
            if (d, e) != (0, 0):
                cp[d, e] = send(
                    src, Pr.at[d, pl.ds(w * q, q)],
                    p_s.at[d * n_w + e], p_r.at[d * n_w + e], (v, sp(d), wp(e)),
                )
    loss = jnp.broadcast_to(log_total - picked, (q, 128))
    loss_o[...] = jnp.transpose(loss)[0:1, :]

    for d, e in plane:
        cp[d, e].wait_recv()
    probs = [jnp.transpose(Pr[d].astype(F32)).astype(BF16) for d in range(n_s)]
    total = part[...]
    for d in range(n_s):
        total = total + lax.dot_general(
            probs[d], H[d], (((1,), (1,)), ((), ())), preferred_element_type=F32
        )
    part[...] = total
    enc[:, :wide], enc[:, wide:] = encode(total)
    cr = {}
    for k in range(1, n_v):
        cr[k] = send(
            enc.at[pl.ds(vp(k) * R, R)], recv.at[k], r_s.at[k], r_r.at[k], (vp(k), s, w)
        )

    cu = {}
    for d in range(1, n_s):
        total = decode(Te[d, pl.ds(v * R, R), :], wide)
        for k in range(1, n_v):
            ct[d, k].wait_recv()
            total = total + decode(Tr[d, k], wide)
        Ue[d, :, :wide], Ue[d, :, wide:] = encode(total)
        cu[d] = send(Ue.at[d], Ur.at[d], u_s.at[d], u_r.at[d], (v, sp(d), w))
    total = part[pl.ds(v * R, R), :]
    for d in range(1, n_s):
        cu[d].wait_recv()
        total = total + decode(Ur[d], wide)
    for k in range(1, n_v):
        cr[k].wait_recv()
        total = total + decode(recv[k], wide)
    grad_o[...] = total
    new_mom = momentum_decay * M[...] + (1.0 - momentum_decay) * total
    square = jnp.sum(new_mom * new_mom, axis=1, keepdims=True)
    sq[...] = jnp.broadcast_to(square, (R, 128))
    cq = {e: send(sq, sqr.at[e], q_s.at[e], q_r.at[e], (v, s, wp(e))) for e in by_reach if e}
    squares = sq[...]
    for e in range(1, n_w):
        cq[e].wait_recv()
        squares = squares + sqr[e]
    factor = step_size / jnp.sqrt(squares[:, 0:1] / (wide * n_w) + epsilon)
    scale_o[...] = jnp.broadcast_to(factor, (R, wide))
    for group in (ce, ch, ct, cl, cp, cr, cu, cq):
        for c in group.values():
            c.wait_send()


def body(hid, emb, mom, ig, rest, tgt, own, row):
    sizes = tuple(lax.axis_size(a) for a in ("vocab", "seq", "width"))
    n_v, n_s, n_w = sizes
    tok, wide = hid.shape
    R = emb.shape[0]
    C, q = n_v * R, tok // n_w
    blocks = n_v * n_s
    room = room_for(wide)
    vmem = pltpu.VMEM
    dma = pltpu.SemaphoreType.DMA
    counts = (n_s, n_v, n_s * n_w, n_s * n_w, n_v, n_s * n_v, n_s, n_w)
    loss, grad, scale = pl.pallas_call(
        functools.partial(kernel, sizes),
        out_shape=(vmem((1, q), F32), vmem((R, wide), F32), vmem((R, wide), F32)),
        in_specs=[pl.BlockSpec(memory_space=pltpu.HBM)] * 8,
        out_specs=[pl.BlockSpec(memory_space=vmem)] * 3,
        scratch_shapes=[
            vmem((blocks, tok), F32),
            vmem((blocks, tok), jnp.int32),
            vmem((blocks, tok), jnp.int32),
            vmem((blocks, tok), jnp.int32),
            vmem((n_s, wide, tok), BF16),
            vmem((wide, tok), BF16),
            vmem((n_v, R, wide), BF16),
            vmem((R, wide), F32),
            vmem((n_s, tok, C), F32),
            vmem((n_s, n_w, q, C), F32),
            vmem((n_s, q, C), BF16),
            vmem((n_s, tok, C), BF16),
            vmem((C, wide), F32),
            vmem((C, room), I16),
            vmem((n_v, R, room), I16),
            vmem((n_s, C, room), I16),
            vmem((n_s, n_v, R, room), I16),
            vmem((n_s, R, room), I16),
            vmem((n_s, R, room), I16),
            vmem((R, 128), F32),
            vmem((n_w, R, 128), F32),
            vmem((tok, tok), jnp.int32),
            vmem((tok, tok), F32),
        ]
        + [dma((n,)) for n in counts for _ in range(2)]
        + [dma((8,)), pltpu.SemaphoreType.REGULAR, pltpu.SemaphoreType.REGULAR],
        compiler_params=pltpu.CompilerParams(
            collective_id=0, has_side_effects=True, vmem_limit_bytes=60 * 2**20
        ),
    )(
        hid.T, emb, mom, ig.T,
        rest.reshape(blocks, tok), tgt.reshape(blocks, tok),
        own.reshape(blocks, tok), row.reshape(blocks, tok),
    )
    new_mom = momentum_decay * mom + (1.0 - momentum_decay) * grad
    new_emb = (emb.astype(F32) - scale * new_mom).astype(BF16)
    return loss.reshape(q), new_mom, new_emb


def solution(mesh):
    placed = P(("vocab", "seq"), "width")
    return jax.shard_map(
        body,
        mesh=mesh,
        in_specs=(placed, placed, placed, placed, P(), P(), P(), P()),
        out_specs=(P(("vocab", "seq", "width")), placed, placed),
        check_vma=False,
    )
```

```python
import functools
import math

import jax
import jax.numpy as jnp
from jax import lax
from jax.experimental import pallas as pl
from jax.experimental.pallas import tpu as pltpu
from jax.sharding import PartitionSpec as P

momentum_decay = 0.75
step_size = 0.1
epsilon = 1e-06
MESH = pl.DeviceIdType.MESH
F32 = jnp.float32
BF16 = jnp.bfloat16
I16 = jnp.int16
TOP = 32704.0
STEPS = 64.0


def column_of(row):
    n = row.shape[1]
    return jnp.transpose(jnp.broadcast_to(row, (n, n)))


def room_for(n):
    return n // 128 * 128 + 128


def scale_of(code):
    return jnp.exp2(code * (1.0 / STEPS))


def encode(x):
    rows, n = x.shape
    largest = jnp.max(jnp.abs(x), axis=1, keepdims=True)
    code = jnp.ceil(jnp.log2(jnp.maximum(largest, 1e-30)) * STEPS) + 1.0
    values = jnp.round(x * (TOP / scale_of(code)))
    return values.astype(jnp.int32).astype(I16), jnp.broadcast_to(
        code, (rows, room_for(n) - n)
    ).astype(jnp.int32).astype(I16)


def decode(x, n):
    code = x[:, n : n + 1].astype(jnp.int32).astype(F32)
    return x[:, :n].astype(jnp.int32).astype(F32) * (scale_of(code) * (1.0 / TOP))


def kernel(
    sizes, hid, emb, mom, ig, rest_h, tgt_h, own_h, row_h, loss_o, grad_o, scale_o,
    rest, tgt, own, row, H, G, E, M, L, Lr, Ps, Pr, part, enc, recv, Te, Tr, Ue, Ur,
    sq, sqr, tcol, rcol,
    h_s, h_r, e_s, e_r, l_s, l_r, p_s, p_r, r_s, r_r, t_s, t_r, u_s, u_r, q_s, q_r, in_s,
    near, far,
):
    n_v, n_s, n_w = sizes
    v, s, w = lax.axis_index("vocab"), lax.axis_index("seq"), lax.axis_index("width")
    wide, tok = hid.shape
    R = emb.shape[0]
    C = n_v * R
    q = tok // n_w
    plane = [(d, e) for d in range(n_s) for e in range(n_w) if (d, e) != (0, 0)]

    by_reach = sorted(range(n_w), key=lambda e: -(e // 2))

    def vp(d):
        return lax.rem(v + d + n_v, n_v)

    def sp(d):
        return lax.rem(s + d + n_s, n_s)

    def wp(e):
        pair = lax.rem(lax.div(w, 2) + e // 2, n_w // 2)
        return pair * 2 + lax.rem(w + e % 2, 2)

    barrier = pltpu.get_barrier_semaphore()
    even = lax.rem(w, 2) == 0
    first, last = w - lax.rem(w, 2), w - lax.rem(w, 2) + 1

    def greet(sem, *device):
        pl.semaphore_signal(sem, inc=1, device_id=device, device_id_type=MESH)

    for d in range(1, n_v):
        greet(barrier, vp(d), s, last)

    @pl.when(even)
    def _():
        greet(barrier, v, s, last)
        for d in range(1, n_s):
            greet(barrier, v, sp(d), first)

    @pl.when(jnp.logical_not(even))
    def _():
        for d in range(n_s):
            greet(barrier, v, sp(d), first)

    for e in range(2, n_w, 2):
        for d in range(n_s):
            greet(barrier, v, sp(d), lax.rem(last + e, n_w))

    local = [
        pltpu.make_async_copy(src, dst, in_s.at[i])
        for i, (src, dst) in enumerate(
            (
                (own_h, own), (row_h, row), (ig, G), (tgt_h, tgt), (rest_h, rest),
                (emb, E.at[v]), (hid, H.at[0]), (mom, M),
            )
        )
    ]
    for c in local:
        c.start()

    def copy(src, dst, ss, rs, dev):
        return pltpu.make_async_remote_copy(
            src_ref=src, dst_ref=dst, send_sem=ss, recv_sem=rs, device_id=dev, device_id_type=MESH
        )

    def order_e():
        turn = (*range(1, n_v), 0)
        found, order = jnp.int32(0), []
        for k in range(n_v - 1):
            found = jnp.maximum(found, (v == turn[k]).astype(jnp.int32))
            order.append((1 - found) * turn[k] + found * turn[k + 1])
        return order

    peers_e = order_e()

    def send(*args):
        c = copy(*args)
        c.start()
        return c

    ch = {d: copy(hid, H.at[d], h_s.at[d], h_r.at[d], (v, sp(d), w)) for d in range(1, n_s)}
    ce = {d: copy(emb, E.at[v], e_s.at[d], e_r.at[v], (peers_e[d - 1], s, w)) for d in range(1, n_v)}

    @pl.when(even)
    def _():
        pl.semaphore_wait(barrier, 2 * n_s - 1)
        greet(near, v, s, last)

    @pl.when(jnp.logical_not(even))
    def _():
        pl.semaphore_wait(near, 1)

    for c in ch.values():
        c.start()

    @pl.when(jnp.logical_not(even))
    def _():
        pl.semaphore_wait(barrier, 2 * n_v - 1 + n_s * (n_w - 2))
        greet(far, v, s, first)

    @pl.when(even)
    def _():
        pl.semaphore_wait(far, 1)

    for c in ce.values():
        c.start()

    mine = v * n_s + s
    r_ids = lax.broadcasted_iota(jnp.int32, (R, tok), 0)
    for c in local[:3]:
        c.wait()
    ids = own[pl.ds(mine, 1), :] * R + row[pl.ds(mine, 1), :]
    scale = math.sqrt(wide * n_w)

    def input_rows(d):
        hot = jnp.concatenate(
            [(r_ids + (k * n_s + sp(d)) * R == ids).astype(F32) for k in range(n_v)], axis=0
        ).astype(BF16)
        return scale * lax.dot_general(
            hot, G[...], (((1,), (1,)), ((), ())), preferred_element_type=F32
        )

    for d in range(1, n_s):
        Te[d, :, :wide], Te[d, :, wide:] = encode(input_rows(d))
    part[...] = input_rows(0)
    for c in local[3:]:
        c.wait()
    tcol[...] = column_of(tgt[pl.ds(mine, 1), :])
    rcol[...] = column_of(rest[pl.ds(mine, 1), :])

    for p in peers_e:
        copy(emb, E.at[p], e_s.at[0], e_r.at[p], (p, s, w)).wait_recv()
    table = E[...].reshape(C, wide)
    cl = {}
    for d in reversed(range(n_s)):
        if d:
            ch[d].wait_recv()
        L[d] = jnp.transpose(jnp.dot(table, H[d], preferred_element_type=F32))
        for e in by_reach:
            if (d, e) != (0, 0):
                cl[d, e] = send(
                    L.at[d, pl.ds(wp(e) * q, q)], Lr.at[d, e],
                    l_s.at[d * n_w + e], l_r.at[d * n_w + e], (v, sp(-d), wp(e)),
                )
    ct = {
        (d, k): send(
            Te.at[d, pl.ds(vp(k) * R, R)], Tr.at[d, k],
            t_s.at[d * n_v + k], t_r.at[d * n_v + k], (vp(k), s, w),
        )
        for d in range(1, n_s)
        for k in range(1, n_v)
    }
    logits = []
    for d in range(n_s):
        total = None
        for e in range(n_w):
            if (d, e) == (0, 0):
                x = L[0, pl.ds(w * q, q), :]
            else:
                cl[d, e].wait_recv()
                x = Lr[d, e]
            total = x if total is None else total + x
        logits.append(total)
    t_col = tcol[pl.ds(w * q, q), 0:1]
    rest_col = rcol[pl.ds(w * q, q), 0:1]
    top = rest_col
    for x in logits:
        top = jnp.maximum(top, jnp.max(x, axis=1, keepdims=True))
    row_sum = jnp.exp(rest_col - top)
    picked = jnp.zeros_like(top)
    lane = lax.broadcasted_iota(jnp.int32, (q, C), 1)
    hits = []
    for d, x in enumerate(logits):
        base = jnp.zeros_like(lane)
        for k in range(n_v):
            base = jnp.where(lane >= k * R, (k * n_s + sp(d)) * R - k * R, base)
        hit = lane + base == t_col
        hits.append(hit)
        row_sum = row_sum + jnp.sum(jnp.exp(x - top), axis=1, keepdims=True)
        picked = picked + jnp.sum(jnp.where(hit, x, 0.0), axis=1, keepdims=True)
    log_total = top + jnp.log(row_sum)
    cp = {}
    for d, x in reversed(list(enumerate(logits))):
        grad = (jnp.exp(x - log_total) - jnp.where(hits[d], 1.0, 0.0)).astype(BF16)
        if d == 0:
            Pr[0, pl.ds(w * q, q), :] = grad
            src = Pr.at[0, pl.ds(w * q, q)]
        else:
            Ps[d] = grad
            src = Ps.at[d]
        for e in by_reach:
            if (d, e) != (0, 0):
                cp[d, e] = send(
                    src, Pr.at[d, pl.ds(w * q, q)],
                    p_s.at[d * n_w + e], p_r.at[d * n_w + e], (v, sp(d), wp(e)),
                )
    loss = jnp.broadcast_to(log_total - picked, (q, 128))
    loss_o[...] = jnp.transpose(loss)[0:1, :]

    for d, e in plane:
        cp[d, e].wait_recv()
    probs = [jnp.transpose(Pr[d].astype(F32)).astype(BF16) for d in range(n_s)]
    total = part[...]
    for d in range(n_s):
        total = total + lax.dot_general(
            probs[d], H[d], (((1,), (1,)), ((), ())), preferred_element_type=F32
        )
    part[...] = total
    enc[:, :wide], enc[:, wide:] = encode(total)
    cr = {}
    for k in range(1, n_v):
        cr[k] = send(
            enc.at[pl.ds(vp(k) * R, R)], recv.at[k], r_s.at[k], r_r.at[k], (vp(k), s, w)
        )

    cu = {}
    for d in range(1, n_s):
        total = decode(Te[d, pl.ds(v * R, R), :], wide)
        for k in range(1, n_v):
            ct[d, k].wait_recv()
            total = total + decode(Tr[d, k], wide)
        Ue[d, :, :wide], Ue[d, :, wide:] = encode(total)
        cu[d] = send(Ue.at[d], Ur.at[d], u_s.at[d], u_r.at[d], (v, sp(d), w))
    total = part[pl.ds(v * R, R), :]
    for d in range(1, n_s):
        cu[d].wait_recv()
        total = total + decode(Ur[d], wide)
    for k in range(1, n_v):
        cr[k].wait_recv()
        total = total + decode(recv[k], wide)
    grad_o[...] = total
    new_mom = momentum_decay * M[...] + (1.0 - momentum_decay) * total
    square = jnp.sum(new_mom * new_mom, axis=1, keepdims=True)
    sq[...] = jnp.broadcast_to(square, (R, 128))
    cq = {e: send(sq, sqr.at[e], q_s.at[e], q_r.at[e], (v, s, wp(e))) for e in by_reach if e}
    squares = sq[...]
    for e in range(1, n_w):
        cq[e].wait_recv()
        squares = squares + sqr[e]
    factor = step_size / jnp.sqrt(squares[:, 0:1] / (wide * n_w) + epsilon)
    scale_o[...] = jnp.broadcast_to(factor, (R, wide))
    for group in (ce, ch, ct, cl, cp, cr, cu, cq):
        for c in group.values():
            c.wait_send()


def body(hid, emb, mom, ig, rest, tgt, own, row):
    sizes = tuple(lax.axis_size(a) for a in ("vocab", "seq", "width"))
    n_v, n_s, n_w = sizes
    tok, wide = hid.shape
    R = emb.shape[0]
    C, q = n_v * R, tok // n_w
    blocks = n_v * n_s
    room = room_for(wide)
    vmem = pltpu.VMEM
    dma = pltpu.SemaphoreType.DMA
    counts = (n_s, n_v, n_s * n_w, n_s * n_w, n_v, n_s * n_v, n_s, n_w)
    loss, grad, scale = pl.pallas_call(
        functools.partial(kernel, sizes),
        out_shape=(vmem((1, q), F32), vmem((R, wide), F32), vmem((R, wide), F32)),
        in_specs=[pl.BlockSpec(memory_space=pltpu.HBM)] * 8,
        out_specs=[pl.BlockSpec(memory_space=vmem)] * 3,
        scratch_shapes=[
            vmem((blocks, tok), F32),
            vmem((blocks, tok), jnp.int32),
            vmem((blocks, tok), jnp.int32),
            vmem((blocks, tok), jnp.int32),
            vmem((n_s, wide, tok), BF16),
            vmem((wide, tok), BF16),
            vmem((n_v, R, wide), BF16),
            vmem((R, wide), F32),
            vmem((n_s, tok, C), F32),
            vmem((n_s, n_w, q, C), F32),
            vmem((n_s, q, C), BF16),
            vmem((n_s, tok, C), BF16),
            vmem((C, wide), F32),
            vmem((C, room), I16),
            vmem((n_v, R, room), I16),
            vmem((n_s, C, room), I16),
            vmem((n_s, n_v, R, room), I16),
            vmem((n_s, R, room), I16),
            vmem((n_s, R, room), I16),
            vmem((R, 128), F32),
            vmem((n_w, R, 128), F32),
            vmem((tok, tok), jnp.int32),
            vmem((tok, tok), F32),
        ]
        + [dma((n,)) for n in counts for _ in range(2)]
        + [dma((8,)), pltpu.SemaphoreType.REGULAR, pltpu.SemaphoreType.REGULAR],
        compiler_params=pltpu.CompilerParams(
            collective_id=0, has_side_effects=True, vmem_limit_bytes=60 * 2**20
        ),
    )(
        hid.T, emb, mom, ig.T,
        rest.reshape(blocks, tok), tgt.reshape(blocks, tok),
        own.reshape(blocks, tok), row.reshape(blocks, tok),
    )
    new_mom = momentum_decay * mom + (1.0 - momentum_decay) * grad
    new_emb = (emb.astype(F32) - scale * new_mom).astype(BF16)
    return loss.reshape(q), new_mom, new_emb


def solution(mesh):
    placed = P(("vocab", "seq"), "width")
    return jax.shard_map(
        body,
        mesh=mesh,
        in_specs=(placed, placed, placed, placed, P(), P(), P(), P()),
        out_specs=(P(("vocab", "seq", "width")), placed, placed),
        check_vma=False,
    )
```
